512 devices in a mesh: image: 16 (over z_hi, x), space: 32 (over z_lo, y, core).
Axes of the slice: x: 4, y: 8, z: 8 (z_hi: 4, z_lo: 2; z = z_hi * 2 + z_lo), core: 2. Of those that a mesh axis runs over, the one named last changes fastest.
Arguments:
- displacement: float32 [16, 3, 32768], P('image', None, 'space'), may hold values from -0.5 to 0.5
- end_states: float32 [2, 3, 32768], P(None, None, 'space'), may hold values from -0.5 to 0.5
- atom_live: int32 [32768], P('space'), may hold values 0 or 1
- partner_cells: int32 [256, 5], P('space'), may hold values from 0 to 11, as said below
- partner_live: int32 [256, 5], P('space'), may hold values from 0 to 1
- spring_const: float32 [16], P('image'), may hold values from 2 to 20
Outputs:
- band_force: float32 [16, 3, 32768], P('image', None, 'space')
- path_stats: float32 [16, 3], P('image')
The draws below stay inside these ranges and needn't reach their ends.
Inputs may be any that keep to these rules, and one draw needn't show every extreme that they name: `partner_cells`: each cell's live entries name the cell itself (index c + 2), the cells c + 1 and c + 3, and for some cells c or c + 4; the live entries are symmetric between cells of the image (counting cells modulo 256); entries come in any order and dead entries name arbitrary cells.
All inputs are finite; a program needn't handle non-finite values. No bound on the sum of `atom_live` on one device may be relied on, other than what follows from the above.
Results may differ from the reference program's by a relative error of at most 0.0003.
Values sent between devices are 32-bit elements; how exact they have to be, the bound alone decides.
No kernel may reach another device: no remote copies, remote signals or barrier semaphores. Data moves between devices by JAX's collectives and lax.ppermute only.
A program may use at most 64 MiB of HBM per device.

```python
import math
import jax
import jax.numpy as jnp
from jax import lax

CELLS = 8
SLOTS = 128
GHOST = 2
ITERATIONS = 6
IMAGES = 16
ALL_CELLS = 256
ATOMS = 32768
N_SPACE = 32


def partner_tables(key):
    cell_ids = jnp.arange(CELLS * N_SPACE, dtype=jnp.int32)
    total_cells = CELLS * N_SPACE
    links = jax.random.randint(jax.random.fold_in(key, 11), (total_cells,), 0, 2).astype(jnp.int32)
    local_ids = cell_ids % CELLS
    offsets = jnp.array([-2, -1, 0, 1, 2], jnp.int32)
    entries = local_ids[:, None] + GHOST + offsets[None, :]
    upper = links[cell_ids]
    lower = links[(cell_ids - 2) % total_cells]
    steady = jnp.ones((total_cells,), jnp.int32)
    used = jnp.stack([lower, steady, steady, steady, upper], axis=1)
    random_cells = jax.random.randint(jax.random.fold_in(key, 12), (total_cells, 5), 0, CELLS + 2 * GHOST).astype(jnp.int32)
    entries = jnp.where(used == 1, entries, random_cells)
    scores = jax.random.randint(jax.random.fold_in(key, 13), (total_cells, 5), 0, 1 << 20).astype(jnp.int32) * 5 + jnp.arange(5, dtype=jnp.int32)[None, :]
    order = jnp.argsort(scores, axis=1)
    entries = jnp.take_along_axis(entries, order, axis=1)
    used = jnp.take_along_axis(used, order, axis=1)
    return (entries.astype(jnp.int32), used.astype(jnp.int32))


def draw_partner_cells(key, part):
    return partner_tables(key)[0]


def draw_partner_live(key, part):
    return partner_tables(key)[1]


def touch_ends(values, stream_key, low, top_value):
    place = [jax.random.randint(jax.random.fold_in(stream_key, axis), (), 0, length) for axis, length in enumerate(values.shape)]
    widest = values.shape.index(max(values.shape))
    beside = place[:widest] + [(place[widest] + 1) % values.shape[widest]] + place[widest + 1:]
    return values.at[tuple(place)].set(low).at[tuple(beside)].set(top_value)


def level_of(own_key, extent, shards, low, high):
    def one(dim, parts):
        steps = jax.random.uniform(jax.random.fold_in(jax.random.fold_in(own_key, 6), dim), (parts,), jnp.float32, low / len(shards), high / len(shards))
        return jnp.repeat(jnp.exp(steps), extent[dim] // parts).reshape((-1,) + (1,) * (len(extent) - dim - 1))

    loudness = one(*shards[0])
    for cut in shards[1:]:
        loudness = loudness * one(*cut)
    return loudness


def gaussian(rng, shape, deviation, bound, shards=(), kind=jnp.bfloat16):
    values = deviation * jax.random.normal(rng, shape, jnp.float32)
    if shards:
        values = values * level_of(rng, shape, shards, -0.22, 0.18)
    return jnp.clip(values, -bound, bound).astype(kind)


def setup_inputs(seed: int = 0) -> dict:
    streams_of = jax.random.split(jax.random.key(seed), 7)
    displacement = gaussian(streams_of[0], (IMAGES, 3, ATOMS), 0.1, 0.5, ((0, 16), (2, 32)), jnp.float32)
    end_states = gaussian(streams_of[1], (2, 3, ATOMS), 0.1, 0.5, ((2, 32),), jnp.float32)
    atom_live = touch_ends((jax.random.randint(streams_of[2], (ATOMS,), 0, 8) < 7).astype(jnp.int32), jax.random.fold_in(streams_of[2], 1), 0, 1)
    partner_cells = draw_partner_cells(jax.random.fold_in(streams_of[6], 71), 0)
    partner_live = draw_partner_live(jax.random.fold_in(streams_of[6], 71), 0)
    spring_const = jnp.clip(jnp.exp(math.log(20.0) - 2.3025851 * jax.random.uniform(streams_of[5], (IMAGES,), jnp.float32) ** level_of(streams_of[5], (IMAGES,), ((0, 16),), -0.2, 0.2)), 2.0, 20.0)
    return dict(displacement=displacement, end_states=end_states, atom_live=atom_live, partner_cells=partner_cells, partner_live=partner_live, spring_const=spring_const)


cutoff_sq = 9.0
pair_strength = 0.4
step_size = 0.02
epsilon = 1e-06
ref_block = 8

def site_table():
    slot_ids = jnp.arange(SLOTS, dtype=jnp.int32)
    return jnp.stack([slot_ids // 64, slot_ids // 8 % 8, slot_ids % 8]).astype(jnp.float32)

def tile_weight(own_live, partner_atoms, tile_live, self_tile, partner):
    diagonal = jnp.arange(SLOTS, dtype=jnp.int32)[:, None] == jnp.arange(SLOTS, dtype=jnp.int32)[None, :]
    weight = own_live[:, :, None] * partner_atoms[:, partner, None, :] * tile_live[:, partner, None, None]
    return jnp.where(self_tile[:, partner, None, None] & diagonal[None], jnp.float32(0.0), weight)

def pair_geometry(own_sites, partner_sites, partner):
    separation = own_sites[:, :, :, None] - partner_sites[:, partner, :, None, :]
    scaled = lax.optimization_barrier(jnp.sum(separation * separation, axis=1)) / cutoff_sq
    remain = jnp.where(scaled < 1.0, 1.0 - scaled, jnp.float32(0.0))
    return (separation, remain)

def density_cells(own_sites, partner_sites, own_live, partner_atoms, tile_live, self_tile):
    density = jnp.zeros(own_live.shape, jnp.float32)
    for partner in range(partner_sites.shape[1]):
        separation, remain = pair_geometry(own_sites, partner_sites, partner)
        weight = tile_weight(own_live, partner_atoms, tile_live, self_tile, partner)
        density = density + lax.optimization_barrier(jnp.sum(weight * remain ** 4, axis=-1))
    return density

def force_cells(own_sites, partner_sites, own_live, partner_atoms, tile_live, self_tile, own_slope, partner_slope):
    total = jnp.zeros(own_sites.shape, jnp.float32)
    for partner in range(partner_sites.shape[1]):
        separation, remain = pair_geometry(own_sites, partner_sites, partner)
        weight = tile_weight(own_live, partner_atoms, tile_live, self_tile, partner)
        slopes = own_slope[:, :, None] + partner_slope[:, partner, None, :]
        coefficient = slopes * (-4.0 * remain ** 3) + pair_strength * (-3.0 * remain ** 2)
        total = total + lax.optimization_barrier(jnp.sum((weight * coefficient)[:, None] * separation, axis=-1))
    return -(2.0 / cutoff_sq) * total

def blocked(function, block_cells, *arrays):
    total_rows = arrays[0].shape[0]
    shaped = tuple((item.reshape((total_rows // block_cells, block_cells) + item.shape[1:]) for item in arrays))
    result = lax.map(lambda group: function(*group), shaped)
    return result.reshape((total_rows,) + result.shape[2:])

def image_forces(moved, live_cells, partner_cells, tile_live):
    cell_disp = moved.reshape(3, ALL_CELLS, SLOTS).transpose(1, 0, 2)
    cell_ids = jnp.arange(ALL_CELLS, dtype=jnp.int32)
    local_ids = cell_ids % CELLS
    targets = (cell_ids[:, None] - local_ids[:, None] + partner_cells - GHOST) % ALL_CELLS
    site = site_table()
    axis_unit = jnp.array([1.0, 0.0, 0.0], jnp.float32)
    own_offset = (2 * (local_ids + GHOST)).astype(jnp.float32)[:, None, None] * axis_unit[None, :, None]
    own_sites = cell_disp + site[None] + own_offset
    part_offset = (2 * partner_cells).astype(jnp.float32)[:, :, None, None] * axis_unit[None, None, :, None]
    partner_sites = cell_disp[targets] + site[None, None] + part_offset
    partner_atoms = live_cells[targets]
    self_tile = partner_cells == (local_ids + GHOST)[:, None]
    density = blocked(density_cells, ref_block, own_sites, partner_sites, live_cells, partner_atoms, tile_live, self_tile)
    slope = -0.5 / jnp.sqrt(1.0 + density) * live_cells
    partner_slope = slope[targets]
    force = blocked(force_cells, ref_block, own_sites, partner_sites, live_cells, partner_atoms, tile_live, self_tile, slope, partner_slope)
    return force.transpose(1, 0, 2).reshape(3, ATOMS)

def reference(displacement, end_states, atom_live, partner_cells, partner_live, spring_const):
    live_flat = atom_live.astype(jnp.float32)
    live_cells = live_flat.reshape(ALL_CELLS, SLOTS)
    tile_live = partner_live.astype(jnp.float32)
    moved = displacement
    for iteration in range(ITERATIONS):
        previous = jnp.concatenate([end_states[0:1], moved[:-1]], axis=0)
        following = jnp.concatenate([moved[1:], end_states[1:2]], axis=0)
        forward_gap = (following - moved) * live_flat
        backward_gap = (moved - previous) * live_flat
        force = lax.map(lambda item: image_forces(item, live_cells, partner_cells, tile_live), moved)
        forward_sq = lax.optimization_barrier(jnp.sum(forward_gap * forward_gap, axis=(1, 2)))
        backward_sq = lax.optimization_barrier(jnp.sum(backward_gap * backward_gap, axis=(1, 2)))
        cross_sum = lax.optimization_barrier(jnp.sum(forward_gap * backward_gap, axis=(1, 2)))
        force_ahead = lax.optimization_barrier(jnp.sum(force * forward_gap, axis=(1, 2)))
        force_behind = lax.optimization_barrier(jnp.sum(force * backward_gap, axis=(1, 2)))
        length_ahead = jnp.sqrt(forward_sq + epsilon)
        length_behind = jnp.sqrt(backward_sq + epsilon)
        tangent_sq = forward_sq / length_ahead ** 2 + backward_sq / length_behind ** 2 + 2.0 * cross_sum / (length_ahead * length_behind)
        tangent_len = jnp.sqrt(jnp.maximum(tangent_sq, 1.0))
        tangent = (forward_gap / length_ahead[:, None, None] + backward_gap / length_behind[:, None, None]) / tangent_len[:, None, None]
        parallel = (force_ahead / length_ahead + force_behind / length_behind) / tangent_len
        spring_term = spring_const * (length_ahead - length_behind)
        band_force = force + (spring_term - parallel)[:, None, None] * tangent
        cosine = cross_sum / (length_ahead * length_behind)
        path_stats = jnp.stack([parallel, spring_term, cosine], axis=-1)
        moved = moved + step_size * band_force
    return (band_force, path_stats)
```

```python
import functools

import jax
import jax.numpy as jnp
from jax import lax
from jax.experimental import pallas as pl
from jax.experimental.pallas import tpu as pltpu
from jax.sharding import PartitionSpec as P


SLOTS = 128
ITERATIONS = 6
CELLS = 8
HALO = 4
WIDE = CELLS + 2 * HALO
OFFSETS = (-2, -1, 0, 1, 2)
DENSE = range(2, WIDE - 2)

cutoff_sq = 9.0
pair_strength = 0.4
step_size = 0.02
epsilon = 1e-06
penalty = 10000.0

f32 = jnp.float32
bf16 = jnp.bfloat16


def vmem(n):
    return [pl.BlockSpec(memory_space=pltpu.VMEM) for _ in range(n)]


def smem():
    return pl.BlockSpec(memory_space=pltpu.SMEM)


def shape(*dims):
    return jax.ShapeDtypeStruct(dims, f32)


def rows_iota():
    return lax.broadcasted_iota(jnp.int32, (8, SLOTS), 0)


def lanes_iota(rows=8):
    return lax.broadcasted_iota(jnp.int32, (rows, SLOTS), 1)


def centred_sites():
    row, lane = rows_iota(), lanes_iota()
    x = (lane // 64).astype(f32) - 0.5
    y = (lane // 8 % 8).astype(f32) - 3.5
    z = (lane % 8).astype(f32) - 3.5
    return jnp.where(row == 0, x, jnp.where(row == 1, y, jnp.where(row == 2, z, 0.0)))


def three_parts(v):
    high = v.astype(bf16).astype(f32)
    rest = v - high
    mid = rest.astype(bf16).astype(f32)
    low = (rest - mid).astype(bf16).astype(f32)
    return high, mid, low


def space_even():
    return 1 - (lax.axis_index("space") & 1)


def pack_kernel(disp, live, cells, used, own, image_out, near_out, far_out):
    even = space_even()
    row = rows_iota()
    lane = lanes_iota()
    cell_id = lax.broadcasted_iota(jnp.int32, cells.shape, 0)
    weight = jnp.zeros((CELLS, SLOTS), f32)
    for n, _ in enumerate(OFFSETS):
        hit = jnp.where(cells[...] == cell_id + n, used[...].astype(f32), 0.0)
        weight = jnp.where(lane == n, jnp.sum(hit, axis=1, keepdims=True), weight)
    for c in range(CELLS):
        part = slice(c * SLOTS, (c + 1) * SLOTS)
        state = jnp.where(row == 3, live[:, part].astype(f32), 0.0)
        state = jnp.where(row == 4, weight[c : c + 1], state)
        for a in range(3):
            state = jnp.where(row == a, disp[a, 0:1, part], state)
        own[c] = state
        image_out[c] = state[0:4]
    near_out[...] = own[pl.ds(even * HALO, HALO)]
    far_out[...] = own[pl.ds((1 - even) * HALO, HALO)]


def join_kernel(own, near, far, wide):
    even = space_even()
    wide[pl.ds(HALO, CELLS)] = own[...]
    wide[pl.ds(even * (HALO + CELLS), HALO)] = near[...]
    wide[pl.ds((1 - even) * (HALO + CELLS), HALO)] = far[...]


def force_kernel(first, *refs):
    if first:
        wide, force, left, right, sums, slope_sums, powers, density = refs
    else:
        base, own, near, far, force = refs[:5]
        left, right, sums, slope_sums, powers, density, wide = refs[5:]
        even = space_even()
        wide[pl.ds(HALO, CELLS)] = own[...]
        wide[pl.ds((1 - even) * (HALO + CELLS), HALO)] = far[...]
        for c in range(HALO):
            at = even * (HALO + CELLS) + c
            wide[at] = jnp.concatenate([near[c], base[at, 4:8]], axis=0)
    row = rows_iota()
    site = centred_sites()

    def placed(c):
        return jnp.where(row < 3, wide[c] + site, 0.0)

    def tall(blocks):
        return jnp.concatenate(blocks, axis=0)

    def squares(p):
        return jnp.sum(p * p, axis=0, keepdims=True) * (1.0 / cutoff_sq)

    def weight_of(c, n):
        return jnp.broadcast_to(wide[c, 4:5, n : n + 1], (1, SLOTS))

    def partner_rows(c):
        p = placed(c)
        alive = wide[c, 3:4, :]
        norm = -squares(p) - penalty * (1.0 - alive)
        rows = p * (2.0 / cutoff_sq)
        rows = jnp.where(row == 3, norm, rows)
        return jnp.where((row == 4) | (row == 6), 1.0, rows)

    def prepare_left(c, _):
        h, m, l = three_parts(partner_rows(c))
        left[c] = tall([h, h, m, m, h, l]).T.astype(bf16)
        sums[c] = tall([h, m, l, jnp.zeros_like(h)]).astype(bf16)
        return 0

    lax.fori_loop(0, WIDE, prepare_left, 0, unroll=8)

    def prepare_right(c, _):
        p = placed(c)
        for n, o in enumerate(OFFSETS):
            q = jnp.where(row == 0, p - 2.0 * o, p)
            rows = jnp.where(row == 3, 1.0, q)
            rows = jnp.where(row == 4, 1.0 - squares(q), rows)
            rows = jnp.where(row == 6, 0.0, rows)
            h, m, l = three_parts(rows)
            right[c, n] = tall([h, m, h, m, l, h]).astype(bf16)
        return 0

    lax.fori_loop(DENSE.start, DENSE.stop, prepare_right, 0, unroll=4)

    def folded(t):
        return jnp.sum(t.reshape(SLOTS // 8, 8, SLOTS), axis=0)

    def two_parts(v):
        high = v.astype(bf16)
        return high, (v - high.astype(f32)).astype(bf16)

    def cell_pair(c, owned):
        total = [jnp.zeros((8, SLOTS), f32), jnp.zeros((8, SLOTS), f32)]
        for dh in range(-2, 4):
            sides = [(i, dh - i + 2) for i in (0, 1) if 0 <= dh - i + 2 < 5]
            blocks = [right[c + i, n] for i, n in sides]
            rhs = blocks[0] if len(blocks) == 1 else jnp.concatenate(blocks, axis=1)
            near = jnp.dot(left[c + dh], rhs, preferred_element_type=f32)
            for b, (i, n) in enumerate(sides):
                t = jnp.maximum(near[:, b * SLOTS : (b + 1) * SLOTS], 0.0)
                square = t * t
                if owned:
                    for k, v in enumerate((square * t, square)):
                        columns = slice(k * SLOTS, (k + 1) * SLOTS)
                        high, low = two_parts(v)
                        at = 2 * n * SLOTS
                        powers[c - HALO + i, at : at + SLOTS, columns] = high
                        powers[c - HALO + i, at + SLOTS : at + 2 * SLOTS, columns] = low
                total[i] = total[i] + weight_of(c + i, n) * folded(square * square)
        for i in (0, 1):
            value = jnp.sum(total[i], axis=0, keepdims=True) - weight_of(c + i, 2)
            alive = wide[c + i, 3:4, :]
            density[c + i] = -0.5 * alive * lax.rsqrt(1.0 + value * alive)

    def rim_pair(k, _):
        cell_pair(2 + 10 * k, False)
        return 0

    def own_pair(k, _):
        cell_pair(HALO + 2 * k, True)
        return 0

    lax.fori_loop(0, 2, rim_pair, 0, unroll=2)
    lax.fori_loop(0, CELLS // 2, own_pair, 0)

    def prepare_slopes(c, _):
        h, m, l = three_parts(partner_rows(c) * density[c])
        slope_sums[c] = tall([h, m, l, jnp.zeros_like(h)]).astype(bf16)
        return 0

    lax.fori_loop(DENSE.start, DENSE.stop, prepare_slopes, 0, unroll=6)

    tilt_row = lax.broadcasted_iota(jnp.int32, (64, SLOTS), 0) % 8 == 6

    def force_cell(k, _):
        c = HALO + k
        parts = []
        for n, o in enumerate(OFFSETS):
            weight = weight_of(c, n)
            factor = jnp.where(tilt_row, o * weight, weight).astype(bf16)
            rows = tall([sums[c + o], slope_sums[c + o]]) * factor
            parts += [rows, rows]
        got = jnp.dot(
            jnp.concatenate(parts, axis=1), powers[k], preferred_element_type=f32
        )

        def joined(at, columns):
            x = got[at : at + 24, columns]
            return x[0:8] + x[8:16] + x[16:24]

        cubes, squared = slice(0, SLOTS), slice(SLOTS, 2 * SLOTS)
        total = (
            -4.0 * (density[c] * joined(0, cubes) + joined(32, cubes))
            - 3.0 * pair_strength * joined(0, squared)
        )
        value = total - (2.0 / cutoff_sq) * placed(c) * total[4:5]
        value = jnp.where(row == 0, value + (4.0 / cutoff_sq) * total[6:7], value)
        force[k] = jnp.where(row < 3, value * wide[c, 3:4, :], 0.0)
        return 0

    lax.fori_loop(0, CELLS, force_cell, 0, unroll=4)


def gaps_kernel(own, force, from_a, from_b, ends, packed, far_out, sums):
    even = space_even()
    image = lax.axis_index("image")
    image_even = 1 - (image & 1)
    edge = (image == 0) | (image == lax.axis_size("image") - 1)
    row = rows_iota()
    kept = row < 3
    blank = jnp.zeros((4, SLOTS), f32)
    totals = [jnp.zeros((8, SLOTS), f32) for _ in range(5)]
    for c in range(CELLS):
        state = own[c]
        alive = state[3:4]
        part = slice(c * SLOTS, (c + 1) * SLOTS)
        both = [jnp.concatenate([ends[a, n : n + 1, part] for a in range(3)], axis=0) for n in (0, 1)]
        fixed = jnp.where(image > 0, both[1], both[0])
        fixed = jnp.concatenate([fixed, blank, blank[0:1]], axis=0)
        one = jnp.concatenate([from_a[c], blank], axis=0)
        other = jnp.concatenate([from_b[c], blank], axis=0)
        other = jnp.where(edge, fixed, other)
        following = jnp.where(image_even == 1, one, other)
        previous = jnp.where(image_even == 1, other, one)
        forward = jnp.where(kept, (following - state) * alive, 0.0)
        backward = jnp.where(kept, (state - previous) * alive, 0.0)
        f = force[c]
        packed[c, 0:8] = f
        packed[c, 8:16] = forward
        packed[c, 16:24] = backward
        pairs = ((forward, forward), (backward, backward), (forward, backward), (f, forward), (f, backward))
        totals = [t + a * b for t, (a, b) in zip(totals, pairs)]
    lane = lanes_iota(1)
    line = jnp.zeros((1, SLOTS), f32)
    for n, t in enumerate(totals):
        value = jnp.sum(jnp.sum(t, axis=0, keepdims=True), axis=1, keepdims=True)
        line = jnp.where(lane == n, value, line)
    sums[...] = jnp.broadcast_to(line[None], sums.shape)
    far_out[...] = packed[pl.ds((1 - even) * HALO, HALO)]


def band_terms(sums, spring):
    total = sums[0]
    for d in range(1, sums.shape[0]):
        total = total + sums[d]

    def value(n):
        return jnp.broadcast_to(total[:, n : n + 1], (1, SLOTS))

    forward_sq, backward_sq, cross, ahead, behind = [value(n) for n in range(5)]
    length_ahead = jnp.sqrt(forward_sq + epsilon)
    length_behind = jnp.sqrt(backward_sq + epsilon)
    both = length_ahead * length_behind
    cosine = cross / both
    tangent_sq = (
        forward_sq / (length_ahead * length_ahead)
        + backward_sq / (length_behind * length_behind)
        + 2.0 * cosine
    )
    tangent_len = jnp.sqrt(jnp.maximum(tangent_sq, 1.0))
    parallel = (ahead / length_ahead + behind / length_behind) / tangent_len
    spring_term = spring * (length_ahead - length_behind)
    pull = (spring_term - parallel) / tangent_len
    return parallel, spring_term, cosine, pull / length_ahead, pull / length_behind


def moved_kernel(spring, sums, old, old_far, packed, far_packed, own, far, image_out, near_out):
    even = space_even()
    _, _, _, ahead, behind = band_terms(sums, spring[0])

    def shifted(state, g):
        return state + step_size * (g[0:8] + ahead * g[8:16] + behind * g[16:24])

    for c in range(CELLS):
        state = shifted(old[c], packed[c])
        own[c] = state
        image_out[c] = state[0:4]
    near_out[...] = image_out[pl.ds(even * HALO, HALO)]
    for c in range(HALO):
        far[c] = shifted(old_far[c], far_packed[c])


def final_kernel(spring, sums, packed, band, stats):
    parallel, spring_term, cosine, ahead, behind = band_terms(sums, spring[0])
    for c in range(CELLS):
        value = packed[c, 0:8] + ahead * packed[c, 8:16] + behind * packed[c, 16:24]
        for a in range(3):
            band[a, 0:1, c * SLOTS : (c + 1) * SLOTS] = value[a : a + 1]
    lane = lanes_iota(1)
    line = jnp.where(lane == 0, parallel, jnp.where(lane == 1, spring_term, cosine))
    stats[...] = line[:, 0:3]


def call(kernel, outs, scalars, arrays, room=2, **more):
    ins = [smem()] * scalars + vmem(arrays)
    return pl.pallas_call(
        kernel,
        out_shape=outs,
        in_specs=ins,
        out_specs=jax.tree.map(lambda _: pl.BlockSpec(memory_space=pltpu.VMEM), outs),
        compiler_params=pltpu.CompilerParams(vmem_limit_bytes=room << 20),
        **more,
    )


def swap_pairs(axis, closed):
    count = lax.axis_size(axis)
    first = [(i, i ^ 1) for i in range(count)]
    second = []
    for i in range(count):
        j = i + 1 if i % 2 else i - 1
        if closed or 0 <= j < count:
            second.append((i, j % count))
    return first, second


def body(displacement, end_states, atom_live, partner_cells, partner_live, spring_const):
    parts = lax.axis_size("space")
    end_states = end_states.transpose(1, 0, 2)
    image_a, image_b = swap_pairs("image", False)
    space_a, space_b = swap_pairs("space", True)

    own, image_out, near, far = call(
        pack_kernel,
        (shape(CELLS, 8, SLOTS), shape(CELLS, 4, SLOTS), shape(HALO, 8, SLOTS), shape(HALO, 8, SLOTS)),
        0,
        4,
    )(displacement.transpose(1, 0, 2), atom_live[None], partner_cells, partner_live)
    near = lax.ppermute(near, "space", space_a)
    far = lax.ppermute(far, "space", space_b)
    base = call(join_kernel, shape(WIDE, 8, SLOTS), 0, 3)(own, near, far)

    def forces(*operands):
        first = len(operands) == 1
        scratch = [
            pltpu.VMEM((WIDE, SLOTS, 48), bf16),
            pltpu.VMEM((WIDE, 5, 48, SLOTS), bf16),
            pltpu.VMEM((WIDE, 32, SLOTS), bf16),
            pltpu.VMEM((WIDE, 32, SLOTS), bf16),
            pltpu.VMEM((CELLS, 10 * SLOTS, 2 * SLOTS), bf16),
            pltpu.VMEM((WIDE, 1, SLOTS), f32),
        ]
        if not first:
            scratch.append(pltpu.VMEM((WIDE, 8, SLOTS), f32))
        return call(
            functools.partial(force_kernel, first),
            shape(CELLS, 8, SLOTS),
            0,
            1 if first else 4,
            room=12,
            scratch_shapes=scratch,
            cost_estimate=pl.CostEstimate(
                flops=20000000, bytes_accessed=200000, transcendentals=2000
            ),
        )(*operands)

    operands = (base,)
    for iteration in range(ITERATIONS):
        from_a = lax.ppermute(image_out, "image", image_a)
        from_b = lax.ppermute(image_out, "image", image_b)
        force = forces(*operands)
        packed, far_packed, sums = call(
            gaps_kernel,
            (shape(CELLS, 24, SLOTS), shape(HALO, 24, SLOTS), shape(parts, 1, SLOTS)),
            0,
            5,
        )(own, force, from_a, from_b, end_states)
        sums = lax.all_to_all(sums, "space", 0, 0, tiled=True)
        if iteration < ITERATIONS - 1:
            far_packed = lax.ppermute(far_packed, "space", space_b)
        if iteration < ITERATIONS - 1:
            own, far, image_out, near = call(
                moved_kernel,
                (
                    shape(CELLS, 8, SLOTS),
                    shape(HALO, 8, SLOTS),
                    shape(CELLS, 4, SLOTS),
                    shape(HALO, 4, SLOTS),
                ),
                1,
                5,
            )(spring_const, sums, own, far, packed, far_packed)
            near = lax.ppermute(near, "space", space_a)
            operands = (base, own, near, far)
    band, stats = call(final_kernel, (shape(3, 1, CELLS * SLOTS), shape(1, 3)), 1, 2)(
        spring_const, sums, packed
    )
    return band.transpose(1, 0, 2), stats


def solution(mesh):
    return jax.shard_map(
        body,
        mesh=mesh,
        in_specs=(
            P("image", None, "space"),
            P(None, None, "space"),
            P("space"),
            P("space", None),
            P("space", None),
            P("image"),
        ),
        out_specs=(P("image", None, "space"), P("image", None)),
        check_vma=False,
    )
```

```python
import functools

import jax
import jax.numpy as jnp
from jax import lax
from jax.experimental import pallas as pl
from jax.experimental.pallas import tpu as pltpu
from jax.sharding import PartitionSpec as P


SLOTS = 128
ITERATIONS = 6
CELLS = 8
HALO = 4
WIDE = CELLS + 2 * HALO
OFFSETS = (-2, -1, 0, 1, 2)
DENSE = range(2, WIDE - 2)

cutoff_sq = 9.0
pair_strength = 0.4
step_size = 0.02
epsilon = 1e-06
penalty = 10000.0

f32 = jnp.float32
bf16 = jnp.bfloat16


def vmem(n):
    return [pl.BlockSpec(memory_space=pltpu.VMEM) for _ in range(n)]


def smem():
    return pl.BlockSpec(memory_space=pltpu.SMEM)


def shape(*dims):
    return jax.ShapeDtypeStruct(dims, f32)


def rows_iota():
    return lax.broadcasted_iota(jnp.int32, (8, SLOTS), 0)


def lanes_iota(rows=8):
    return lax.broadcasted_iota(jnp.int32, (rows, SLOTS), 1)


def centred_sites():
    row, lane = rows_iota(), lanes_iota()
    x = (lane // 64).astype(f32) - 0.5
    y = (lane // 8 % 8).astype(f32) - 3.5
    z = (lane % 8).astype(f32) - 3.5
    return jnp.where(row == 0, x, jnp.where(row == 1, y, jnp.where(row == 2, z, 0.0)))


def three_parts(v):
    high = v.astype(bf16).astype(f32)
    rest = v - high
    mid = rest.astype(bf16).astype(f32)
    low = (rest - mid).astype(bf16).astype(f32)
    return high, mid, low


def space_even():
    return 1 - (lax.axis_index("space") & 1)


def pack_kernel(*refs):
    own, image_out, near_out, far_out = refs[4:8]
    done = refs[12]
    copies = [
        pltpu.make_async_copy(source, target, done.at[n])
        for n, (source, target) in enumerate(zip(refs[:4], refs[8:12]))
    ]
    for copy in copies:
        copy.start()
    for copy in copies:
        copy.wait()
    disp, live, cells, used = refs[8:12]
    even = space_even()
    row = rows_iota()
    lane = lanes_iota()
    cell_id = lax.broadcasted_iota(jnp.int32, cells.shape, 0)
    weight = jnp.zeros((CELLS, SLOTS), f32)
    for n, _ in enumerate(OFFSETS):
        hit = jnp.where(cells[...] == cell_id + n, used[...].astype(f32), 0.0)
        weight = jnp.where(lane == n, jnp.sum(hit, axis=1, keepdims=True), weight)
    for c in range(CELLS):
        part = slice(c * SLOTS, (c + 1) * SLOTS)
        state = jnp.where(row == 3, live[:, part].astype(f32), 0.0)
        state = jnp.where(row == 4, weight[c : c + 1], state)
        for a in range(3):
            state = jnp.where(row == a, disp[a, 0:1, part], state)
        own[c] = state
        image_out[c] = state[0:4]
    near_out[...] = own[pl.ds(even * HALO, HALO)]
    far_out[...] = own[pl.ds((1 - even) * HALO, HALO)]


def join_kernel(own, near, far, wide):
    even = space_even()
    wide[pl.ds(HALO, CELLS)] = own[...]
    wide[pl.ds(even * (HALO + CELLS), HALO)] = near[...]
    wide[pl.ds((1 - even) * (HALO + CELLS), HALO)] = far[...]


def force_kernel(first, *refs):
    if first:
        wide, force, left, right, sums, slopes, tiles, density = refs
    else:
        base, own, near, far, force = refs[:5]
        left, right, sums, slopes, tiles, density, wide = refs[5:]
        even = space_even()
        wide[pl.ds(HALO, CELLS)] = own[...]
        wide[pl.ds((1 - even) * (HALO + CELLS), HALO)] = far[...]
        for c in range(HALO):
            at = even * (HALO + CELLS) + c
            wide[at] = jnp.concatenate([near[c], base[at, 4:8]], axis=0)
    row = rows_iota()
    site = centred_sites()

    def placed(c):
        return jnp.where(row < 3, wide[c] + site, 0.0)

    def tall(blocks):
        return jnp.concatenate(blocks, axis=0)

    def squares(p):
        return jnp.sum(p * p, axis=0, keepdims=True) * (1.0 / cutoff_sq)

    def weight_of(c, n):
        return jnp.broadcast_to(wide[c, 4:5, n : n + 1], (1, SLOTS))

    def partner_rows(c):
        p = placed(c)
        alive = wide[c, 3:4, :]
        norm = -squares(p) - penalty * (1.0 - alive)
        rows = p * (2.0 / cutoff_sq)
        rows = jnp.where(row == 3, norm, rows)
        return jnp.where((row == 4) | (row == 6), 1.0, rows)

    def prepare_left(c, _):
        h, m, l = three_parts(partner_rows(c))
        left[c] = tall([h, h, m, m, h, l]).T.astype(bf16)
        sums[c] = tall([h, m, l, jnp.zeros_like(h)]).astype(bf16)
        return 0

    lax.fori_loop(0, WIDE, prepare_left, 0, unroll=16)

    def prepare_right(c, _):
        p = placed(c)
        for n, o in enumerate(OFFSETS):
            q = jnp.where(row == 0, p - 2.0 * o, p)
            rows = jnp.where(row == 3, 1.0, q)
            rows = jnp.where(row == 4, 1.0 - squares(q), rows)
            rows = jnp.where(row == 6, 0.0, rows)
            h, m, l = three_parts(rows)
            right[c, n] = tall([h, m, h, m, l, h]).astype(bf16)
        return 0

    lax.fori_loop(DENSE.start, DENSE.stop, prepare_right, 0, unroll=12)

    def folded(t):
        return jnp.sum(t.reshape(SLOTS // 8, 8, SLOTS), axis=0)

    def cell_pair(c, owned):
        total = [jnp.zeros((8, SLOTS), f32), jnp.zeros((8, SLOTS), f32)]
        for dh in range(-2, 4):
            sides = [(i, dh - i + 2) for i in (0, 1) if 0 <= dh - i + 2 < 5]
            blocks = [right[c + i, n] for i, n in sides]
            rhs = blocks[0] if len(blocks) == 1 else jnp.concatenate(blocks, axis=1)
            near = jnp.dot(left[c + dh], rhs, preferred_element_type=f32)
            for b, (i, n) in enumerate(sides):
                t = jnp.maximum(near[:, b * SLOTS : (b + 1) * SLOTS], 0.0)
                if owned:
                    tiles[c - HALO + i, n] = t
                square = t * t
                total[i] = total[i] + weight_of(c + i, n) * folded(square * square)
        for i in (0, 1):
            value = jnp.sum(total[i], axis=0, keepdims=True) - weight_of(c + i, 2)
            alive = wide[c + i, 3:4, :]
            density[c + i] = -0.5 * alive * lax.rsqrt(1.0 + value * alive)

    def rim_pair(k, _):
        cell_pair(2 + 10 * k, False)
        return 0

    def own_pair(k, _):
        cell_pair(HALO + 2 * k, True)
        return 0

    lax.fori_loop(0, 2, rim_pair, 0, unroll=2)
    lax.fori_loop(0, CELLS // 2, own_pair, 0, unroll=4)

    def prepare_slopes(c, _):
        slope = -4.0 * density[c]
        high = slope.astype(bf16).astype(f32)
        rest = (slope - high).astype(bf16).astype(f32)
        lines = jnp.where(row == 0, high, jnp.where(row == 1, rest, 0.0))
        column = tall([lines, jnp.zeros_like(lines)]).T.astype(bf16)
        slopes[c] = jnp.dot(column, jnp.ones((16, SLOTS), bf16), preferred_element_type=f32)
        return 0

    lax.fori_loop(DENSE.start, DENSE.stop, prepare_slopes, 0, unroll=12)

    def force_pair(k, _):
        c = HALO + 2 * k
        total = [jnp.zeros((8, SLOTS), f32), jnp.zeros((8, SLOTS), f32)]
        tilt = [jnp.zeros((8, SLOTS), f32), jnp.zeros((8, SLOTS), f32)]
        ours = [-4.0 * density[c], -4.0 * density[c + 1]]
        for dh in range(-2, 4):
            sides = [(i, dh - i + 2) for i in (0, 1) if 0 <= dh - i + 2 < 5]
            highs, lows = [], []
            for i, n in sides:
                t = tiles[2 * k + i, n]
                value = t * t * ((slopes[c + dh] + ours[i]) * t - 3.0 * pair_strength)
                high = value.astype(bf16)
                highs.append(high)
                lows.append((value - high.astype(f32)).astype(bf16))
            got = jnp.dot(
                jnp.concatenate([sums[c + dh]] * 2, axis=1),
                tall([jnp.concatenate(v, axis=1) if len(v) > 1 else v[0] for v in (highs, lows)]),
                preferred_element_type=f32,
            )
            for b, (i, n) in enumerate(sides):
                part = got[:, b * SLOTS : (b + 1) * SLOTS]
                part = weight_of(c + i, n) * (part[0:8] + part[8:16] + part[16:24])
                total[i] = total[i] + part
                if OFFSETS[n]:
                    tilt[i] = tilt[i] + (4.0 * OFFSETS[n] / cutoff_sq) * part
        for i in (0, 1):
            value = total[i] - (2.0 / cutoff_sq) * placed(c + i) * total[i][4:5]
            value = jnp.where(row == 0, value + tilt[i][4:5], value)
            force[2 * k + i] = jnp.where(row < 3, value * wide[c + i, 3:4, :], 0.0)
        return 0

    lax.fori_loop(0, CELLS // 2, force_pair, 0, unroll=4)


def gaps_kernel(own, force, from_a, from_b, ends, packed, sums, far_out=None):
    image = lax.axis_index("image")
    image_even = 1 - (image & 1)
    edge = (image == 0) | (image == lax.axis_size("image") - 1)
    row = rows_iota()
    kept = row < 3
    blank = jnp.zeros((4, SLOTS), f32)
    totals = [jnp.zeros((8, SLOTS), f32) for _ in range(5)]
    for c in range(CELLS):
        state = own[c]
        alive = state[3:4]
        part = slice(c * SLOTS, (c + 1) * SLOTS)
        both = [jnp.concatenate([ends[a, n : n + 1, part] for a in range(3)], axis=0) for n in (0, 1)]
        fixed = jnp.where(image > 0, both[1], both[0])
        fixed = jnp.concatenate([fixed, blank, blank[0:1]], axis=0)
        one = jnp.concatenate([from_a[c], blank], axis=0)
        other = jnp.concatenate([from_b[c], blank], axis=0)
        other = jnp.where(edge, fixed, other)
        following = jnp.where(image_even == 1, one, other)
        previous = jnp.where(image_even == 1, other, one)
        forward = jnp.where(kept, (following - state) * alive, 0.0)
        backward = jnp.where(kept, (state - previous) * alive, 0.0)
        f = force[c]
        packed[c, 0:8] = f
        packed[c, 8:16] = forward
        packed[c, 16:24] = backward
        pairs = ((forward, forward), (backward, backward), (forward, backward), (f, forward), (f, backward))
        totals = [t + a * b for t, (a, b) in zip(totals, pairs)]
    lane = lanes_iota(1)
    line = jnp.zeros((1, SLOTS), f32)
    for n, t in enumerate(totals):
        value = jnp.sum(jnp.sum(t, axis=0, keepdims=True), axis=1, keepdims=True)
        line = jnp.where(lane == n, value, line)
    sums[...] = jnp.broadcast_to(line[None], sums.shape)
    if far_out is not None:
        far_out[...] = packed[pl.ds((1 - space_even()) * HALO, HALO)]


def band_terms(sums, spring):
    total = sums[0]
    for d in range(1, sums.shape[0]):
        total = total + sums[d]

    def value(n):
        return jnp.broadcast_to(total[:, n : n + 1], (1, SLOTS))

    forward_sq, backward_sq, cross, ahead, behind = [value(n) for n in range(5)]
    length_ahead = jnp.sqrt(forward_sq + epsilon)
    length_behind = jnp.sqrt(backward_sq + epsilon)
    both = length_ahead * length_behind
    cosine = cross / both
    tangent_sq = (
        forward_sq / (length_ahead * length_ahead)
        + backward_sq / (length_behind * length_behind)
        + 2.0 * cosine
    )
    tangent_len = jnp.sqrt(jnp.maximum(tangent_sq, 1.0))
    parallel = (ahead / length_ahead + behind / length_behind) / tangent_len
    spring_term = spring * (length_ahead - length_behind)
    pull = (spring_term - parallel) / tangent_len
    return parallel, spring_term, cosine, pull / length_ahead, pull / length_behind


def moved_kernel(spring, sums, old, old_far, packed, far_packed, own, far, image_out, near_out):
    even = space_even()
    _, _, _, ahead, behind = band_terms(sums, spring[0])

    def shifted(state, g):
        return state + step_size * (g[0:8] + ahead * g[8:16] + behind * g[16:24])

    for c in range(CELLS):
        state = shifted(old[c], packed[c])
        own[c] = state
        image_out[c] = state[0:4]
    near_out[...] = image_out[pl.ds(even * HALO, HALO)]
    for c in range(HALO):
        far[c] = shifted(old_far[c], far_packed[c])


def final_kernel(spring, sums, packed, band, stats):
    parallel, spring_term, cosine, ahead, behind = band_terms(sums, spring[0])
    for c in range(CELLS):
        value = packed[c, 0:8] + ahead * packed[c, 8:16] + behind * packed[c, 16:24]
        for a in range(3):
            band[a, 0:1, c * SLOTS : (c + 1) * SLOTS] = value[a : a + 1]
    lane = lanes_iota(1)
    line = jnp.where(lane == 0, parallel, jnp.where(lane == 1, spring_term, cosine))
    stats[...] = line[:, 0:3]


def call(kernel, outs, scalars, arrays, room=2, **more):
    ins = [smem()] * scalars + vmem(arrays)
    return pl.pallas_call(
        kernel,
        out_shape=outs,
        in_specs=ins,
        out_specs=jax.tree.map(lambda _: pl.BlockSpec(memory_space=pltpu.VMEM), outs),
        compiler_params=pltpu.CompilerParams(vmem_limit_bytes=room << 20),
        **more,
    )


def swap_pairs(axis, closed):
    count = lax.axis_size(axis)
    first = [(i, i ^ 1) for i in range(count)]
    second = []
    for i in range(count):
        j = i + 1 if i % 2 else i - 1
        if closed or 0 <= j < count:
            second.append((i, j % count))
    return first, second


def body(displacement, end_states, atom_live, partner_cells, partner_live, spring_const):
    parts = lax.axis_size("space")
    end_states = end_states.transpose(1, 0, 2)
    image_a, image_b = swap_pairs("image", False)
    space_a, space_b = swap_pairs("space", True)

    raw = (displacement.transpose(1, 0, 2), atom_live[None], partner_cells, partner_live)
    outs = (
        shape(CELLS, 8, SLOTS),
        shape(CELLS, 4, SLOTS),
        shape(HALO, 8, SLOTS),
        shape(HALO, 8, SLOTS),
    )
    own, image_out, near, far = pl.pallas_call(
        pack_kernel,
        out_shape=outs,
        in_specs=[pl.BlockSpec(memory_space=pltpu.HBM)] * 4,
        out_specs=tuple(vmem(4)),
        scratch_shapes=[pltpu.VMEM(v.shape, v.dtype) for v in raw]
        + [pltpu.SemaphoreType.DMA((4,))],
        name="pack",
        compiler_params=pltpu.CompilerParams(vmem_limit_bytes=62 << 20),
    )(*raw)
    near = lax.ppermute(near, "space", space_a)
    far = lax.ppermute(far, "space", space_b)
    base = call(join_kernel, shape(WIDE, 8, SLOTS), 0, 3)(own, near, far)

    def forces(*operands):
        first = len(operands) == 1
        scratch = [
            pltpu.VMEM((WIDE, SLOTS, 48), bf16),
            pltpu.VMEM((WIDE, 5, 48, SLOTS), bf16),
            pltpu.VMEM((WIDE, 32, SLOTS), bf16),
            pltpu.VMEM((WIDE, SLOTS, SLOTS), f32),
            pltpu.VMEM((CELLS, 5, SLOTS, SLOTS), f32),
            pltpu.VMEM((WIDE, 1, SLOTS), f32),
        ]
        if not first:
            scratch.append(pltpu.VMEM((WIDE, 8, SLOTS), f32))
        return call(
            functools.partial(force_kernel, first),
            shape(CELLS, 8, SLOTS),
            0,
            1 if first else 4,
            room=12,
            scratch_shapes=scratch,
            cost_estimate=pl.CostEstimate(
                flops=20000000, bytes_accessed=200000, transcendentals=2000
            ),
        )(*operands)

    operands = (base,)
    for iteration in range(ITERATIONS):
        from_a = lax.ppermute(image_out, "image", image_a)
        from_b = lax.ppermute(image_out, "image", image_b)
        force = forces(*operands)
        more = iteration < ITERATIONS - 1
        packed, sums, *far_packed = call(
            gaps_kernel,
            (shape(CELLS, 24, SLOTS), shape(parts, 1, SLOTS))
            + (shape(HALO, 24, SLOTS),) * more,
            0,
            5,
        )(own, force, from_a, from_b, end_states)
        sums = lax.all_to_all(sums, "space", 0, 0, tiled=True)
        if more:
            far_packed = lax.ppermute(far_packed[0], "space", space_b)
        if more:
            own, far, image_out, near = call(
                moved_kernel,
                (
                    shape(CELLS, 8, SLOTS),
                    shape(HALO, 8, SLOTS),
                    shape(CELLS, 4, SLOTS),
                    shape(HALO, 4, SLOTS),
                ),
                1,
                5,
            )(spring_const, sums, own, far, packed, far_packed)
            near = lax.ppermute(near, "space", space_a)
            operands = (base, own, near, far)
    band, stats = call(final_kernel, (shape(3, 1, CELLS * SLOTS), shape(1, 3)), 1, 2)(
        spring_const, sums, packed
    )
    return band.transpose(1, 0, 2), stats


def solution(mesh):
    return jax.shard_map(
        body,
        mesh=mesh,
        in_specs=(
            P("image", None, "space"),
            P(None, None, "space"),
            P("space"),
            P("space", None),
            P("space", None),
            P("image"),
        ),
        out_specs=(P("image", None, "space"), P("image", None)),
        check_vma=False,
    )
```

```python
import functools

import jax
import jax.numpy as jnp
from jax import lax
from jax.experimental import pallas as pl
from jax.experimental.pallas import tpu as pltpu
from jax.sharding import PartitionSpec as P


SLOTS = 128
ITERATIONS = 6
CELLS = 8
HALO = 4
WIDE = CELLS + 2 * HALO
OFFSETS = (-2, -1, 0, 1, 2)
DENSE = range(2, WIDE - 2)

cutoff_sq = 9.0
pair_strength = 0.4
step_size = 0.02
epsilon = 1e-06
penalty = 10000.0

f32 = jnp.float32
bf16 = jnp.bfloat16


def vmem(n):
    return [pl.BlockSpec(memory_space=pltpu.VMEM) for _ in range(n)]


def smem():
    return pl.BlockSpec(memory_space=pltpu.SMEM)


def shape(*dims):
    return jax.ShapeDtypeStruct(dims, f32)


def rows_iota():
    return lax.broadcasted_iota(jnp.int32, (8, SLOTS), 0)


def lanes_iota(rows=8):
    return lax.broadcasted_iota(jnp.int32, (rows, SLOTS), 1)


def centred_sites():
    row, lane = rows_iota(), lanes_iota()
    x = (lane // 64).astype(f32) - 0.5
    y = (lane // 8 % 8).astype(f32) - 3.5
    z = (lane % 8).astype(f32) - 3.5
    return jnp.where(row == 0, x, jnp.where(row == 1, y, jnp.where(row == 2, z, 0.0)))


def three_parts(v):
    high = v.astype(bf16).astype(f32)
    rest = v - high
    mid = rest.astype(bf16).astype(f32)
    low = (rest - mid).astype(bf16).astype(f32)
    return high, mid, low


def space_even():
    return 1 - (lax.axis_index("space") & 1)


def pack_kernel(*refs):
    own, image_out, near_out, far_out = refs[4:8]
    done = refs[12]
    copies = [
        pltpu.make_async_copy(source, target, done.at[n])
        for n, (source, target) in enumerate(zip(refs[:4], refs[8:12]))
    ]
    for copy in copies:
        copy.start()
    for copy in copies:
        copy.wait()
    disp, live, cells, used = refs[8:12]
    even = space_even()
    row = rows_iota()
    lane = lanes_iota()
    cell_id = lax.broadcasted_iota(jnp.int32, cells.shape, 0)
    weight = jnp.zeros((CELLS, SLOTS), f32)
    for n, _ in enumerate(OFFSETS):
        hit = jnp.where(cells[...] == cell_id + n, used[...].astype(f32), 0.0)
        weight = jnp.where(lane == n, jnp.sum(hit, axis=1, keepdims=True), weight)
    for c in range(CELLS):
        part = slice(c * SLOTS, (c + 1) * SLOTS)
        state = jnp.where(row == 3, live[:, part].astype(f32), 0.0)
        state = jnp.where(row == 4, weight[c : c + 1], state)
        for a in range(3):
            state = jnp.where(row == a, disp[a, 0:1, part], state)
        own[c] = state
        image_out[c] = state[0:4]
    near_out[...] = own[pl.ds(even * HALO, HALO)]
    far_out[...] = own[pl.ds((1 - even) * HALO, HALO)]


def join_kernel(own, near, far, wide):
    even = space_even()
    wide[pl.ds(HALO, CELLS)] = own[...]
    wide[pl.ds(even * (HALO + CELLS), HALO)] = near[...]
    wide[pl.ds((1 - even) * (HALO + CELLS), HALO)] = far[...]


def force_kernel(first, *refs):
    if first:
        wide, force, left, right, sums, slopes, tiles, density = refs
    else:
        base, own, near, far, force = refs[:5]
        left, right, sums, slopes, tiles, density, wide = refs[5:]
        even = space_even()
        wide[pl.ds(HALO, CELLS)] = own[...]
        wide[pl.ds((1 - even) * (HALO + CELLS), HALO)] = far[...]
        for c in range(HALO):
            at = even * (HALO + CELLS) + c
            wide[at] = jnp.concatenate([near[c], base[at, 4:8]], axis=0)
    row = rows_iota()
    site = centred_sites()

    def placed(c):
        return jnp.where(row < 3, wide[c] + site, 0.0)

    def tall(blocks):
        return jnp.concatenate(blocks, axis=0)

    def squares(p):
        return jnp.sum(p * p, axis=0, keepdims=True) * (1.0 / cutoff_sq)

    def weight_of(c, n):
        return jnp.broadcast_to(wide[c, 4:5, n : n + 1], (1, SLOTS))

    def partner_rows(c):
        p = placed(c)
        alive = wide[c, 3:4, :]
        norm = -squares(p) - penalty * (1.0 - alive)
        rows = p * (2.0 / cutoff_sq)
        rows = jnp.where(row == 3, norm, rows)
        return jnp.where((row == 4) | (row == 6), 1.0, rows)

    def prepare_left(c, _):
        h, m, l = three_parts(partner_rows(c))
        left[c] = tall([h, h, m, m, h, l]).T.astype(bf16)
        sums[c] = tall([h, m, l, jnp.zeros_like(h)]).astype(bf16)
        return 0

    lax.fori_loop(0, WIDE, prepare_left, 0, unroll=16)

    def prepare_right(c, _):
        p = placed(c)
        for n, o in enumerate(OFFSETS):
            q = jnp.where(row == 0, p - 2.0 * o, p)
            rows = jnp.where(row == 3, 1.0, q)
            rows = jnp.where(row == 4, 1.0 - squares(q), rows)
            rows = jnp.where(row == 6, 0.0, rows)
            h, m, l = three_parts(rows)
            right[c, n] = tall([h, m, h, m, l, h]).astype(bf16)
        return 0

    lax.fori_loop(DENSE.start, DENSE.stop, prepare_right, 0, unroll=12)

    def folded(t):
        return jnp.sum(t.reshape(SLOTS // 8, 8, SLOTS), axis=0)

    def cell_pair(c, owned):
        total = [jnp.zeros((8, SLOTS), f32), jnp.zeros((8, SLOTS), f32)]
        for dh in range(-2, 4):
            sides = [(i, dh - i + 2) for i in (0, 1) if 0 <= dh - i + 2 < 5]
            blocks = [right[c + i, n] for i, n in sides]
            rhs = blocks[0] if len(blocks) == 1 else jnp.concatenate(blocks, axis=1)
            near = jnp.dot(left[c + dh], rhs, preferred_element_type=f32)
            for b, (i, n) in enumerate(sides):
                t = jnp.maximum(near[:, b * SLOTS : (b + 1) * SLOTS], 0.0)
                if owned:
                    tiles[c - HALO + i, n] = t
                square = t * t
                total[i] = total[i] + weight_of(c + i, n) * folded(square * square)
        for i in (0, 1):
            value = jnp.sum(total[i], axis=0, keepdims=True) - weight_of(c + i, 2)
            alive = wide[c + i, 3:4, :]
            density[c + i] = -0.5 * alive * lax.rsqrt(1.0 + value * alive)

    def rim_pair(k, _):
        cell_pair(2 + 10 * k, False)
        return 0

    def own_pair(k, _):
        cell_pair(HALO + 2 * k, True)
        return 0

    lax.fori_loop(0, 2, rim_pair, 0, unroll=2)
    lax.fori_loop(0, CELLS // 2, own_pair, 0, unroll=4)

    def prepare_slopes(c, _):
        slope = -4.0 * density[c]
        high = slope.astype(bf16).astype(f32)
        rest = (slope - high).astype(bf16).astype(f32)
        lines = jnp.where(row == 0, high, jnp.where(row == 1, rest, 0.0))
        column = tall([lines, jnp.zeros_like(lines)]).T.astype(bf16)
        slopes[c] = jnp.dot(column, jnp.ones((16, SLOTS), bf16), preferred_element_type=f32)
        return 0

    lax.fori_loop(DENSE.start, DENSE.stop, prepare_slopes, 0, unroll=12)

    def force_pair(k, _):
        c = HALO + 2 * k
        total = [jnp.zeros((8, SLOTS), f32), jnp.zeros((8, SLOTS), f32)]
        tilt = [jnp.zeros((8, SLOTS), f32), jnp.zeros((8, SLOTS), f32)]
        ours = [-4.0 * density[c], -4.0 * density[c + 1]]
        for dh in range(-2, 4):
            sides = [(i, dh - i + 2) for i in (0, 1) if 0 <= dh - i + 2 < 5]
            highs, lows = [], []
            for i, n in sides:
                t = tiles[2 * k + i, n]
                value = t * t * ((slopes[c + dh] + ours[i]) * t - 3.0 * pair_strength)
                high = value.astype(bf16)
                highs.append(high)
                lows.append((value - high.astype(f32)).astype(bf16))
            got = jnp.dot(
                jnp.concatenate([sums[c + dh]] * 2, axis=1),
                tall([jnp.concatenate(v, axis=1) if len(v) > 1 else v[0] for v in (highs, lows)]),
                preferred_element_type=f32,
            )
            for b, (i, n) in enumerate(sides):
                part = got[:, b * SLOTS : (b + 1) * SLOTS]
                part = weight_of(c + i, n) * (part[0:8] + part[8:16] + part[16:24])
                total[i] = total[i] + part
                if OFFSETS[n]:
                    tilt[i] = tilt[i] + (4.0 * OFFSETS[n] / cutoff_sq) * part
        for i in (0, 1):
            value = total[i] - (2.0 / cutoff_sq) * placed(c + i) * total[i][4:5]
            value = jnp.where(row == 0, value + tilt[i][4:5], value)
            force[2 * k + i] = jnp.where(row < 3, value * wide[c + i, 3:4, :], 0.0)
        return 0

    lax.fori_loop(0, CELLS // 2, force_pair, 0, unroll=4)


def gaps_kernel(own, force, from_a, from_b, ends, packed, sums, far_out=None):
    image = lax.axis_index("image")
    image_even = 1 - (image & 1)
    edge = (image == 0) | (image == lax.axis_size("image") - 1)
    row = rows_iota()
    kept = row < 3
    blank = jnp.zeros((4, SLOTS), f32)
    totals = [jnp.zeros((8, SLOTS), f32) for _ in range(5)]
    for c in range(CELLS):
        state = own[c]
        alive = state[3:4]
        part = slice(c * SLOTS, (c + 1) * SLOTS)
        both = [jnp.concatenate([ends[a, n : n + 1, part] for a in range(3)], axis=0) for n in (0, 1)]
        fixed = jnp.where(image > 0, both[1], both[0])
        fixed = jnp.concatenate([fixed, blank, blank[0:1]], axis=0)
        one = jnp.concatenate([from_a[c], blank], axis=0)
        other = jnp.concatenate([from_b[c], blank], axis=0)
        other = jnp.where(edge, fixed, other)
        following = jnp.where(image_even == 1, one, other)
        previous = jnp.where(image_even == 1, other, one)
        forward = jnp.where(kept, (following - state) * alive, 0.0)
        backward = jnp.where(kept, (state - previous) * alive, 0.0)
        f = force[c]
        packed[c, 0:8] = f
        packed[c, 8:16] = forward
        packed[c, 16:24] = backward
        pairs = ((forward, forward), (backward, backward), (forward, backward), (f, forward), (f, backward))
        totals = [t + a * b for t, (a, b) in zip(totals, pairs)]
    lane = lanes_iota(1)
    line = jnp.zeros((1, SLOTS), f32)
    for n, t in enumerate(totals):
        value = jnp.sum(jnp.sum(t, axis=0, keepdims=True), axis=1, keepdims=True)
        line = jnp.where(lane == n, value, line)
    sums[...] = jnp.broadcast_to(line[None], sums.shape)
    if far_out is not None:
        start = (1 - space_even()) * HALO
        for c in range(HALO):
            for n in range(3):
                far_out[c, n] = packed[start + c, 8 * n : 8 * n + 4]


def band_terms(sums, spring):
    total = sums[0]
    for d in range(1, sums.shape[0]):
        total = total + sums[d]

    def value(n):
        return jnp.broadcast_to(total[:, n : n + 1], (1, SLOTS))

    forward_sq, backward_sq, cross, ahead, behind = [value(n) for n in range(5)]
    length_ahead = jnp.sqrt(forward_sq + epsilon)
    length_behind = jnp.sqrt(backward_sq + epsilon)
    both = length_ahead * length_behind
    cosine = cross / both
    tangent_sq = (
        forward_sq / (length_ahead * length_ahead)
        + backward_sq / (length_behind * length_behind)
        + 2.0 * cosine
    )
    tangent_len = jnp.sqrt(jnp.maximum(tangent_sq, 1.0))
    parallel = (ahead / length_ahead + behind / length_behind) / tangent_len
    spring_term = spring * (length_ahead - length_behind)
    pull = (spring_term - parallel) / tangent_len
    return parallel, spring_term, cosine, pull / length_ahead, pull / length_behind


def moved_kernel(spring, sums, old, old_far, packed, far_packed, own, far, image_out, near_out):
    even = space_even()
    _, _, _, ahead, behind = band_terms(sums, spring[0])

    def shifted(state, f, forward, backward):
        return state + step_size * (f + ahead * forward + behind * backward)

    for c in range(CELLS):
        state = shifted(old[c], *[packed[c, 8 * n : 8 * n + 8] for n in range(3)])
        own[c] = state
        image_out[c] = state[0:4]
    near_out[...] = image_out[pl.ds(even * HALO, HALO)]
    for c in range(HALO):
        rim = [far_packed[c, n] for n in range(3)]
        far[c] = jnp.concatenate([shifted(old_far[c, 0:4], *rim), old_far[c, 4:8]], axis=0)


def final_kernel(spring, sums, packed, band, stats):
    parallel, spring_term, cosine, ahead, behind = band_terms(sums, spring[0])
    for c in range(CELLS):
        value = packed[c, 0:8] + ahead * packed[c, 8:16] + behind * packed[c, 16:24]
        for a in range(3):
            band[a, 0:1, c * SLOTS : (c + 1) * SLOTS] = value[a : a + 1]
    lane = lanes_iota(1)
    line = jnp.where(lane == 0, parallel, jnp.where(lane == 1, spring_term, cosine))
    stats[...] = line[:, 0:3]


def call(kernel, outs, scalars, arrays, room=2, **more):
    ins = [smem()] * scalars + vmem(arrays)
    return pl.pallas_call(
        kernel,
        out_shape=outs,
        in_specs=ins,
        out_specs=jax.tree.map(lambda _: pl.BlockSpec(memory_space=pltpu.VMEM), outs),
        compiler_params=pltpu.CompilerParams(vmem_limit_bytes=room << 20),
        **more,
    )


def swap_pairs(axis, closed):
    count = lax.axis_size(axis)
    first = [(i, i ^ 1) for i in range(count)]
    second = []
    for i in range(count):
        j = i + 1 if i % 2 else i - 1
        if closed or 0 <= j < count:
            second.append((i, j % count))
    return first, second


def body(displacement, end_states, atom_live, partner_cells, partner_live, spring_const):
    parts = lax.axis_size("space")
    end_states = end_states.transpose(1, 0, 2)
    image_a, image_b = swap_pairs("image", False)
    space_a, space_b = swap_pairs("space", True)

    raw = (displacement.transpose(1, 0, 2), atom_live[None], partner_cells, partner_live)
    outs = (
        shape(CELLS, 8, SLOTS),
        shape(CELLS, 4, SLOTS),
        shape(HALO, 8, SLOTS),
        shape(HALO, 8, SLOTS),
    )
    own, image_out, near, far = pl.pallas_call(
        pack_kernel,
        out_shape=outs,
        in_specs=[pl.BlockSpec(memory_space=pltpu.HBM)] * 4,
        out_specs=tuple(vmem(4)),
        scratch_shapes=[pltpu.VMEM(v.shape, v.dtype) for v in raw]
        + [pltpu.SemaphoreType.DMA((4,))],
        name="pack",
        compiler_params=pltpu.CompilerParams(vmem_limit_bytes=2 << 20),
    )(*[pltpu.with_memory_space_constraint(v, pltpu.HBM) for v in raw])
    near = lax.ppermute(near, "space", space_a)
    far = lax.ppermute(far, "space", space_b)
    base = call(join_kernel, shape(WIDE, 8, SLOTS), 0, 3)(own, near, far)

    def forces(*operands):
        first = len(operands) == 1
        scratch = [
            pltpu.VMEM((WIDE, SLOTS, 48), bf16),
            pltpu.VMEM((WIDE, 5, 48, SLOTS), bf16),
            pltpu.VMEM((WIDE, 32, SLOTS), bf16),
            pltpu.VMEM((WIDE, SLOTS, SLOTS), f32),
            pltpu.VMEM((CELLS, 5, SLOTS, SLOTS), f32),
            pltpu.VMEM((WIDE, 1, SLOTS), f32),
        ]
        if not first:
            scratch.append(pltpu.VMEM((WIDE, 8, SLOTS), f32))
        return call(
            functools.partial(force_kernel, first),
            shape(CELLS, 8, SLOTS),
            0,
            1 if first else 4,
            room=12,
            scratch_shapes=scratch,
            cost_estimate=pl.CostEstimate(
                flops=20000000, bytes_accessed=200000, transcendentals=2000
            ),
        )(*operands)

    operands = (base,)
    for iteration in range(ITERATIONS):
        from_a = lax.ppermute(image_out, "image", image_a)
        from_b = lax.ppermute(image_out, "image", image_b)
        force = forces(*operands)
        more = iteration < ITERATIONS - 1
        packed, sums, *far_packed = call(
            gaps_kernel,
            (shape(CELLS, 24, SLOTS), shape(parts, 1, SLOTS))
            + (shape(HALO, 3, 4, SLOTS),) * more,
            0,
            5,
        )(own, force, from_a, from_b, end_states)
        sums = lax.all_to_all(sums, "space", 0, 0, tiled=True)
        if more:
            far_packed = lax.ppermute(far_packed[0], "space", space_b)
        if more:
            own, far, image_out, near = call(
                moved_kernel,
                (
                    shape(CELLS, 8, SLOTS),
                    shape(HALO, 8, SLOTS),
                    shape(CELLS, 4, SLOTS),
                    shape(HALO, 4, SLOTS),
                ),
                1,
                5,
            )(spring_const, sums, own, far, packed, far_packed)
            near = lax.ppermute(near, "space", space_a)
            operands = (base, own, near, far)
    band, stats = call(final_kernel, (shape(3, 1, CELLS * SLOTS), shape(1, 3)), 1, 2)(
        spring_const, sums, packed
    )
    return band.transpose(1, 0, 2), stats


def solution(mesh):
    return jax.shard_map(
        body,
        mesh=mesh,
        in_specs=(
            P("image", None, "space"),
            P(None, None, "space"),
            P("space"),
            P("space", None),
            P("space", None),
            P("image"),
        ),
        out_specs=(P("image", None, "space"), P("image", None)),
        check_vma=False,
    )
```

```python
import functools

import jax
import jax.numpy as jnp
from jax import lax
from jax.experimental import pallas as pl
from jax.experimental.pallas import tpu as pltpu
from jax.sharding import PartitionSpec as P


SLOTS = 128
ITERATIONS = 6
CELLS = 8
HALO = 4
WIDE = CELLS + 2 * HALO
OFFSETS = (-2, -1, 0, 1, 2)
DENSE = range(2, WIDE - 2)

cutoff_sq = 9.0
pair_strength = 0.4
step_size = 0.02
epsilon = 1e-06
penalty = 10000.0

f32 = jnp.float32
bf16 = jnp.bfloat16


def vmem(n):
    return [pl.BlockSpec(memory_space=pltpu.VMEM) for _ in range(n)]


def smem():
    return pl.BlockSpec(memory_space=pltpu.SMEM)


def shape(*dims):
    return jax.ShapeDtypeStruct(dims, f32)


def rows_iota():
    return lax.broadcasted_iota(jnp.int32, (8, SLOTS), 0)


def lanes_iota(rows=8):
    return lax.broadcasted_iota(jnp.int32, (rows, SLOTS), 1)


def centred_sites():
    row, lane = rows_iota(), lanes_iota()
    x = (lane // 64).astype(f32) - 0.5
    y = (lane // 8 % 8).astype(f32) - 3.5
    z = (lane % 8).astype(f32) - 3.5
    return jnp.where(row == 0, x, jnp.where(row == 1, y, jnp.where(row == 2, z, 0.0)))


def three_parts(v):
    high = v.astype(bf16).astype(f32)
    rest = v - high
    mid = rest.astype(bf16).astype(f32)
    low = (rest - mid).astype(bf16).astype(f32)
    return high, mid, low


def space_even():
    return 1 - (lax.axis_index("space") & 1)


def pack_kernel(*refs):
    own, image_out, near_out, far_out = refs[4:8]
    done = refs[12]
    copies = [
        pltpu.make_async_copy(source, target, done.at[n])
        for n, (source, target) in enumerate(zip(refs[:4], refs[8:12]))
    ]
    for copy in copies:
        copy.start()
    for copy in copies:
        copy.wait()
    disp, live, cells, used = refs[8:12]
    even = space_even()
    row = rows_iota()
    lane = lanes_iota()
    cell_id = lax.broadcasted_iota(jnp.int32, cells.shape, 0)
    weight = jnp.zeros((CELLS, SLOTS), f32)
    for n, _ in enumerate(OFFSETS):
        hit = jnp.where(cells[...] == cell_id + n, used[...].astype(f32), 0.0)
        weight = jnp.where(lane == n, jnp.sum(hit, axis=1, keepdims=True), weight)
    for c in range(CELLS):
        part = slice(c * SLOTS, (c + 1) * SLOTS)
        state = jnp.where(row == 3, live[:, part].astype(f32), 0.0)
        state = jnp.where(row == 4, weight[c : c + 1], state)
        for a in range(3):
            state = jnp.where(row == a, disp[a, 0:1, part], state)
        own[c] = state
        image_out[c] = state[0:4]
    near_out[...] = own[pl.ds(even * HALO, HALO)]
    far_out[...] = own[pl.ds((1 - even) * HALO, HALO)]


def join_kernel(own, near, far, wide):
    even = space_even()
    wide[pl.ds(HALO, CELLS)] = own[...]
    wide[pl.ds(even * (HALO + CELLS), HALO)] = near[...]
    wide[pl.ds((1 - even) * (HALO + CELLS), HALO)] = far[...]


def force_kernel(first, *refs):
    if first:
        wide, force, left, right, sums, slopes, tiles, density = refs
    else:
        own, near, far, force = refs[:4]
        left, right, sums, slopes, tiles, density, wide = refs[4:]
        even = space_even()
        wide[pl.ds(HALO, CELLS)] = own[...]
        wide[pl.ds(even * (HALO + CELLS), HALO)] = near[...]
        wide[pl.ds((1 - even) * (HALO + CELLS), HALO)] = far[...]
    row = rows_iota()
    site = centred_sites()

    def placed(c):
        return jnp.where(row < 3, wide[c] + site, 0.0)

    def tall(blocks):
        return jnp.concatenate(blocks, axis=0)

    def squares(p):
        return jnp.sum(p * p, axis=0, keepdims=True) * (1.0 / cutoff_sq)

    def weight_of(c, n):
        return jnp.broadcast_to(wide[c, 4:5, n : n + 1], (1, SLOTS))

    def partner_rows(c):
        p = placed(c)
        alive = wide[c, 3:4, :]
        norm = -squares(p) - penalty * (1.0 - alive)
        rows = p * (2.0 / cutoff_sq)
        rows = jnp.where(row == 3, norm, rows)
        return jnp.where((row == 4) | (row == 6), 1.0, rows)

    def prepare_left(c, _):
        h, m, l = three_parts(partner_rows(c))
        left[c] = tall([h, h, m, m, h, l]).T.astype(bf16)
        sums[c] = tall([h, m, l, jnp.zeros_like(h)]).astype(bf16)
        return 0

    lax.fori_loop(0, WIDE, prepare_left, 0, unroll=16)

    def prepare_right(c, _):
        p = placed(c)
        for n, o in enumerate(OFFSETS):
            q = jnp.where(row == 0, p - 2.0 * o, p)
            rows = jnp.where(row == 3, 1.0, q)
            rows = jnp.where(row == 4, 1.0 - squares(q), rows)
            rows = jnp.where(row == 6, 0.0, rows)
            h, m, l = three_parts(rows)
            right[c, n] = tall([h, m, h, m, l, h]).astype(bf16)
        return 0

    lax.fori_loop(DENSE.start, DENSE.stop, prepare_right, 0, unroll=12)

    def folded(t):
        return jnp.sum(t.reshape(SLOTS // 8, 8, SLOTS), axis=0)

    def cell_pair(c, owned):
        total = [jnp.zeros((8, SLOTS), f32), jnp.zeros((8, SLOTS), f32)]
        for dh in range(-2, 4):
            sides = [(i, dh - i + 2) for i in (0, 1) if 0 <= dh - i + 2 < 5]
            blocks = [right[c + i, n] for i, n in sides]
            rhs = blocks[0] if len(blocks) == 1 else jnp.concatenate(blocks, axis=1)
            near = jnp.dot(left[c + dh], rhs, preferred_element_type=f32)
            for b, (i, n) in enumerate(sides):
                t = jnp.maximum(near[:, b * SLOTS : (b + 1) * SLOTS], 0.0)
                if owned:
                    tiles[c - HALO + i, n] = t
                square = t * t
                total[i] = total[i] + weight_of(c + i, n) * folded(square * square)
        for i in (0, 1):
            value = jnp.sum(total[i], axis=0, keepdims=True) - weight_of(c + i, 2)
            alive = wide[c + i, 3:4, :]
            density[c + i] = -0.5 * alive * lax.rsqrt(1.0 + value * alive)

    def rim_pair(k, _):
        cell_pair(2 + 10 * k, False)
        return 0

    def own_pair(k, _):
        cell_pair(HALO + 2 * k, True)
        return 0

    lax.fori_loop(0, 2, rim_pair, 0, unroll=2)
    lax.fori_loop(0, CELLS // 2, own_pair, 0, unroll=4)

    def prepare_slopes(c, _):
        slope = -4.0 * density[c]
        high = slope.astype(bf16).astype(f32)
        rest = (slope - high).astype(bf16).astype(f32)
        lines = jnp.where(row == 0, high, jnp.where(row == 1, rest, 0.0))
        column = tall([lines, jnp.zeros_like(lines)]).T.astype(bf16)
        slopes[c] = jnp.dot(column, jnp.ones((16, SLOTS), bf16), preferred_element_type=f32)
        return 0

    lax.fori_loop(DENSE.start, DENSE.stop, prepare_slopes, 0, unroll=12)

    def force_pair(k, _):
        c = HALO + 2 * k
        total = [jnp.zeros((8, SLOTS), f32), jnp.zeros((8, SLOTS), f32)]
        tilt = [jnp.zeros((8, SLOTS), f32), jnp.zeros((8, SLOTS), f32)]
        ours = [-4.0 * density[c], -4.0 * density[c + 1]]
        for dh in range(-2, 4):
            sides = [(i, dh - i + 2) for i in (0, 1) if 0 <= dh - i + 2 < 5]
            highs, lows = [], []
            for i, n in sides:
                t = tiles[2 * k + i, n]
                value = t * t * ((slopes[c + dh] + ours[i]) * t - 3.0 * pair_strength)
                high = value.astype(bf16)
                highs.append(high)
                lows.append((value - high.astype(f32)).astype(bf16))
            got = jnp.dot(
                jnp.concatenate([sums[c + dh]] * 2, axis=1),
                tall([jnp.concatenate(v, axis=1) if len(v) > 1 else v[0] for v in (highs, lows)]),
                preferred_element_type=f32,
            )
            for b, (i, n) in enumerate(sides):
                part = got[:, b * SLOTS : (b + 1) * SLOTS]
                part = weight_of(c + i, n) * (part[0:8] + part[8:16] + part[16:24])
                total[i] = total[i] + part
                if OFFSETS[n]:
                    tilt[i] = tilt[i] + (4.0 * OFFSETS[n] / cutoff_sq) * part
        for i in (0, 1):
            value = total[i] - (2.0 / cutoff_sq) * placed(c + i) * total[i][4:5]
            value = jnp.where(row == 0, value + tilt[i][4:5], value)
            force[2 * k + i] = jnp.where(row < 3, value * wide[c + i, 3:4, :], 0.0)
        return 0

    lax.fori_loop(0, CELLS // 2, force_pair, 0, unroll=4)


def gaps_kernel(own, force, from_a, from_b, ends, packed, sums, near_out=None, far_out=None):
    image = lax.axis_index("image")
    image_even = 1 - (image & 1)
    edge = (image == 0) | (image == lax.axis_size("image") - 1)
    row = rows_iota()
    kept = row < 3
    blank = jnp.zeros((4, SLOTS), f32)
    totals = [jnp.zeros((8, SLOTS), f32) for _ in range(5)]
    for c in range(CELLS):
        state = own[c]
        alive = state[3:4]
        part = slice(c * SLOTS, (c + 1) * SLOTS)
        both = [jnp.concatenate([ends[a, n : n + 1, part] for a in range(3)], axis=0) for n in (0, 1)]
        fixed = jnp.where(image > 0, both[1], both[0])
        fixed = jnp.concatenate([fixed, blank, blank[0:1]], axis=0)
        one = jnp.concatenate([from_a[c], blank], axis=0)
        other = jnp.concatenate([from_b[c], blank], axis=0)
        other = jnp.where(edge, fixed, other)
        following = jnp.where(image_even == 1, one, other)
        previous = jnp.where(image_even == 1, other, one)
        forward = jnp.where(kept, (following - state) * alive, 0.0)
        backward = jnp.where(kept, (state - previous) * alive, 0.0)
        f = force[c]
        packed[c, 0:8] = f
        packed[c, 8:16] = forward
        packed[c, 16:24] = backward
        pairs = ((forward, forward), (backward, backward), (forward, backward), (f, forward), (f, backward))
        totals = [t + a * b for t, (a, b) in zip(totals, pairs)]
    lane = lanes_iota(1)
    line = jnp.zeros((1, SLOTS), f32)
    for n, t in enumerate(totals):
        value = jnp.sum(jnp.sum(t, axis=0, keepdims=True), axis=1, keepdims=True)
        line = jnp.where(lane == n, value, line)
    sums[...] = jnp.broadcast_to(line[None], sums.shape)
    if far_out is not None:
        start = space_even() * HALO
        for c in range(HALO):
            for n in range(3):
                near_out[c, n] = packed[start + c, 8 * n : 8 * n + 4]
                far_out[c, n] = packed[HALO - start + c, 8 * n : 8 * n + 4]


def band_terms(sums, spring):
    total = sums[0]
    for d in range(1, sums.shape[0]):
        total = total + sums[d]

    def value(n):
        return jnp.broadcast_to(total[:, n : n + 1], (1, SLOTS))

    forward_sq, backward_sq, cross, ahead, behind = [value(n) for n in range(5)]
    length_ahead = jnp.sqrt(forward_sq + epsilon)
    length_behind = jnp.sqrt(backward_sq + epsilon)
    both = length_ahead * length_behind
    cosine = cross / both
    tangent_sq = (
        forward_sq / (length_ahead * length_ahead)
        + backward_sq / (length_behind * length_behind)
        + 2.0 * cosine
    )
    tangent_len = jnp.sqrt(jnp.maximum(tangent_sq, 1.0))
    parallel = (ahead / length_ahead + behind / length_behind) / tangent_len
    spring_term = spring * (length_ahead - length_behind)
    pull = (spring_term - parallel) / tangent_len
    return parallel, spring_term, cosine, pull / length_ahead, pull / length_behind


def moved_kernel(spring, sums, old, old_near, old_far, packed, near_packed, far_packed, *outs):
    own, near, far, image_out = outs
    _, _, _, ahead, behind = band_terms(sums, spring[0])

    def shifted(state, f, forward, backward):
        return state + step_size * (f + ahead * forward + behind * backward)

    for c in range(CELLS):
        state = shifted(old[c], *[packed[c, 8 * n : 8 * n + 8] for n in range(3)])
        own[c] = state
        image_out[c] = state[0:4]
    for halo, old_halo, halo_packed in ((near, old_near, near_packed), (far, old_far, far_packed)):
        for c in range(HALO):
            rim = [halo_packed[c, n] for n in range(3)]
            state = old_halo[c]
            halo[c] = jnp.concatenate([shifted(state[0:4], *rim), state[4:8]], axis=0)


def final_kernel(spring, sums, packed, band, stats):
    parallel, spring_term, cosine, ahead, behind = band_terms(sums, spring[0])
    for c in range(CELLS):
        value = packed[c, 0:8] + ahead * packed[c, 8:16] + behind * packed[c, 16:24]
        for a in range(3):
            band[a, 0:1, c * SLOTS : (c + 1) * SLOTS] = value[a : a + 1]
    lane = lanes_iota(1)
    line = jnp.where(lane == 0, parallel, jnp.where(lane == 1, spring_term, cosine))
    stats[...] = line[:, 0:3]


def call(kernel, outs, scalars, arrays, room=2, **more):
    ins = [smem()] * scalars + vmem(arrays)
    return pl.pallas_call(
        kernel,
        out_shape=outs,
        in_specs=ins,
        out_specs=jax.tree.map(lambda _: pl.BlockSpec(memory_space=pltpu.VMEM), outs),
        compiler_params=pltpu.CompilerParams(vmem_limit_bytes=room << 20),
        **more,
    )


def swap_pairs(axis, closed):
    count = lax.axis_size(axis)
    first = [(i, i ^ 1) for i in range(count)]
    second = []
    for i in range(count):
        j = i + 1 if i % 2 else i - 1
        if closed or 0 <= j < count:
            second.append((i, j % count))
    return first, second


def body(displacement, end_states, atom_live, partner_cells, partner_live, spring_const):
    parts = lax.axis_size("space")
    end_states = end_states.transpose(1, 0, 2)
    image_a, image_b = swap_pairs("image", False)
    space_a, space_b = swap_pairs("space", True)

    raw = (displacement.transpose(1, 0, 2), atom_live[None], partner_cells, partner_live)
    outs = (
        shape(CELLS, 8, SLOTS),
        shape(CELLS, 4, SLOTS),
        shape(HALO, 8, SLOTS),
        shape(HALO, 8, SLOTS),
    )
    own, image_out, near, far = pl.pallas_call(
        pack_kernel,
        out_shape=outs,
        in_specs=[pl.BlockSpec(memory_space=pltpu.HBM)] * 4,
        out_specs=tuple(vmem(4)),
        scratch_shapes=[pltpu.VMEM(v.shape, v.dtype) for v in raw]
        + [pltpu.SemaphoreType.DMA((4,))],
        name="pack",
        compiler_params=pltpu.CompilerParams(vmem_limit_bytes=2 << 20),
    )(*[pltpu.with_memory_space_constraint(v, pltpu.HBM) for v in raw])
    near = lax.ppermute(near, "space", space_a)
    far = lax.ppermute(far, "space", space_b)
    base = call(join_kernel, shape(WIDE, 8, SLOTS), 0, 3)(own, near, far)

    def forces(*operands):
        first = len(operands) == 1
        scratch = [
            pltpu.VMEM((WIDE, SLOTS, 48), bf16),
            pltpu.VMEM((WIDE, 5, 48, SLOTS), bf16),
            pltpu.VMEM((WIDE, 32, SLOTS), bf16),
            pltpu.VMEM((WIDE, SLOTS, SLOTS), f32),
            pltpu.VMEM((CELLS, 5, SLOTS, SLOTS), f32),
            pltpu.VMEM((WIDE, 1, SLOTS), f32),
        ]
        if not first:
            scratch.append(pltpu.VMEM((WIDE, 8, SLOTS), f32))
        return call(
            functools.partial(force_kernel, first),
            shape(CELLS, 8, SLOTS),
            0,
            1 if first else 3,
            room=12,
            scratch_shapes=scratch,
            cost_estimate=pl.CostEstimate(
                flops=20000000, bytes_accessed=200000, transcendentals=2000
            ),
        )(*operands)

    operands = (base,)
    for iteration in range(ITERATIONS):
        from_a = lax.ppermute(image_out, "image", image_a)
        from_b = lax.ppermute(image_out, "image", image_b)
        force = forces(*operands)
        more = iteration < ITERATIONS - 1
        packed, sums, *rims = call(
            gaps_kernel,
            (shape(CELLS, 24, SLOTS), shape(parts, 1, SLOTS))
            + (shape(HALO, 3, 4, SLOTS),) * (2 * more),
            0,
            5,
        )(own, force, from_a, from_b, end_states)
        sums = lax.all_to_all(sums, "space", 0, 0, tiled=True)
        if more:
            near_packed = lax.ppermute(rims[0], "space", space_a)
            far_packed = lax.ppermute(rims[1], "space", space_b)
        if more:
            own, near, far, image_out = call(
                moved_kernel,
                (
                    shape(CELLS, 8, SLOTS),
                    shape(HALO, 8, SLOTS),
                    shape(HALO, 8, SLOTS),
                    shape(CELLS, 4, SLOTS),
                ),
                1,
                7,
            )(spring_const, sums, own, near, far, packed, near_packed, far_packed)
            operands = (own, near, far)
    band, stats = call(final_kernel, (shape(3, 1, CELLS * SLOTS), shape(1, 3)), 1, 2)(
        spring_const, sums, packed
    )
    return band.transpose(1, 0, 2), stats


def solution(mesh):
    return jax.shard_map(
        body,
        mesh=mesh,
        in_specs=(
            P("image", None, "space"),
            P(None, None, "space"),
            P("space"),
            P("space", None),
            P("space", None),
            P("image"),
        ),
        out_specs=(P("image", None, "space"), P("image", None)),
        check_vma=False,
    )
```
